128 devices in a mesh: lat: 4 (over x_hi, core), lon: 32 (over y, x_lo, z).
Axes of the slice: x: 4 (x_hi: 2, x_lo: 2; x = x_hi * 2 + x_lo), y: 4, z: 4, core: 2. Of those that a mesh axis runs over, the one named last changes fastest.
Arguments:
- inputs: bfloat16 [32, 10240, 512], P('lat', 'lon'), may hold values from -6 to 6
- w_conv: bfloat16 [512, 512], replicated, may hold values from -0.25 to 0.25
- w_point: bfloat16 [512, 512], replicated, may hold values from -0.25 to 0.25
- cotangent: bfloat16 [32, 2560, 512], P('lat', 'lon'), may hold values from -6 to 6
Outputs:
- encoded: bfloat16 [32, 2560, 512], P('lat', 'lon')
- grad_inputs: bfloat16 [32, 10240, 512], P('lat', 'lon')
- grad_conv: float32 [512, 512], P(None, ('lat', 'lon'))
- grad_point: float32 [512, 512], P(None, ('lat', 'lon'))
The draws below stay inside these ranges and needn't reach their ends.
All inputs are finite; a program needn't handle non-finite values.
Results may differ from the reference program's by a relative error of at most 0.005.
Values may be sent and summed in bfloat16 or wider, within the bound.
A program may use at most 128 MiB of HBM per device.

```python
import math
import jax
import jax.numpy as jnp
from jax import lax

C = 512
G = 8
KW = 8
GROUP = 64
LAT = 32
LON = 10240
LON_OUT = 2560
POSITIONS = 81920


def raised(drawn, stream_key, source, target, shards_of, factor):
    owner, partner = [(jnp.arange(drawn.shape[position]) // (drawn.shape[position] // shards_of)).reshape([-1 if axis == position else 1 for axis in range(drawn.ndim)]) for position in (source, target)]
    chosen = jax.random.permutation(stream_key, shards_of)[partner]
    strong = (owner == chosen) | (owner == (partner + shards_of // 2) % shards_of)
    return jnp.where(strong, factor * drawn, drawn)


def level_of(rng, extent, split, smallest, top_value):
    def one(position, parts):
        steps = jax.random.uniform(jax.random.fold_in(jax.random.fold_in(rng, 6), position), (parts,), jnp.float32, smallest / len(split), top_value / len(split))
        return jnp.repeat(jnp.exp(steps), extent[position] // parts).reshape((-1,) + (1,) * (len(extent) - position - 1))

    level = one(*split[0])
    for cut in split[1:]:
        level = level * one(*cut)
    return level


def gaussian(stream_key, dims, scale, reach, shards=(), kind=jnp.bfloat16):
    gain = level_of(stream_key, dims, shards, -0.22, 0.18) if shards else 1.0
    values = jax.random.normal(stream_key, dims, jnp.float32) * scale * gain
    return jnp.minimum(jnp.maximum(values, -reach), reach).astype(kind)


def gaussian_with(key, shape, scale, limit, pieces, heavy, held_as=jnp.bfloat16):
    entries = scale * jax.random.normal(key, shape, jnp.float32)
    if pieces:
        entries = entries * level_of(key, shape, pieces, -0.22, 0.18)
    return jnp.clip(raised(entries, jax.random.fold_in(key, 3), *heavy), -limit, limit).astype(held_as)


def setup_inputs(seed: int = 0) -> dict:
    splits = jax.random.split(jax.random.key(seed), 5)
    return {
        "inputs": gaussian(splits[0], (LAT, LON, C), 1.0, 6.0, ((0, 4), (1, 32))),
        "w_conv": gaussian(splits[1], (KW * GROUP, C), (KW * GROUP) ** -0.5, 0.25),
        "w_point": gaussian(splits[2], (C, C), C ** -0.5, 0.25),
        "cotangent": gaussian_with(splits[3], (LAT, LON_OUT, C), 1.0, 6.0, ((0, 4), (1, 32)), (0, 2, 4, 2.0)),
    }


def reference(inputs, w_conv, w_point, cotangent):
    kernel = w_conv.astype(jnp.float32).reshape(KW, GROUP, G, GROUP)

    def row_step(carry, pair):
        input_row, cot_row = pair
        padded = jnp.concatenate([input_row[LON - 2:], input_row, input_row[:2]], 0)
        leading = padded[:LON].reshape(LON_OUT, 4, C)
        trailing = padded[4:LON + 4].reshape(LON_OUT, 4, C)
        patches = jnp.concatenate([leading, trailing], 1).reshape(LON_OUT, KW, G, GROUP).astype(jnp.float32)
        preact = jnp.einsum('pkgi,kigo->pgo', patches, kernel).reshape(LON_OUT, C)
        activated, gelu_back = jax.vjp(jax.nn.gelu, preact)
        act_bf = activated.astype(jnp.bfloat16)
        encoded_row = jnp.dot(act_bf, w_point, preferred_element_type=jnp.float32).astype(jnp.bfloat16)
        point_part = jnp.dot(act_bf.T, cot_row, preferred_element_type=jnp.float32)
        act_grad = jnp.dot(cot_row, w_point.T, preferred_element_type=jnp.float32)
        pre_grad = gelu_back(act_grad)[0].astype(jnp.bfloat16)
        pre_split = pre_grad.astype(jnp.float32).reshape(LON_OUT, G, GROUP)
        conv_part = jnp.einsum('pkgi,pgo->kigo', patches, pre_split).reshape(KW * GROUP, C)
        patch_grad = jnp.einsum('pgo,kigo->pkgi', pre_split, kernel).reshape(LON_OUT, KW, C)
        front = patch_grad[:, :4].reshape(LON, C)
        behind = patch_grad[:, 4:].reshape(LON, C)
        zeros_four = jnp.zeros((4, C), jnp.float32)
        extended = jnp.concatenate([front, zeros_four], 0) + jnp.concatenate([zeros_four, behind], 0)
        middle = extended[2:LON + 2]
        grad_row = jnp.concatenate([middle[:2] + extended[LON + 2:], middle[2:LON - 2], middle[LON - 2:] + extended[:2]], 0)
        new_carry = (carry[0] + conv_part, carry[1] + point_part)
        return (new_carry, (encoded_row, grad_row.astype(jnp.bfloat16)))
    start = (jnp.zeros((KW * GROUP, C), jnp.float32), jnp.zeros((C, C), jnp.float32))
    sums, outputs = lax.scan(row_step, start, (inputs, cotangent))
    grad_scale = 1.0 / math.sqrt(POSITIONS)
    return (outputs[0], outputs[1], sums[0] * grad_scale, sums[1] * grad_scale)
```

```python
import functools
import math

import jax
import jax.numpy as jnp
from jax import lax
from jax.experimental import pallas as pl
from jax.experimental.pallas import tpu as pltpu
from jax.sharding import PartitionSpec as P

MESH = pl.DeviceIdType.MESH
F32 = jnp.float32
BF16 = jnp.bfloat16
G = 8
KW = 8
C = 512
HALF = 256
GELU_C = math.sqrt(2.0 / math.pi)
GELU_A = 0.044715


def nt_dot(a, b):
    return lax.dot_general(a, b, (((1,), (1,)), ((), ())), preferred_element_type=F32)


def dot(a, b):
    return jnp.dot(a, b, preferred_element_type=F32)


def messages(rows8):
    low = lax.broadcasted_iota(jnp.int32, (8, 128), 0) < 4
    tiles = [rows8[:, l * 128 : (l + 1) * 128] for l in range(4)]
    rolled = [pltpu.roll(t, 4, 0) for t in tiles]
    even = [jnp.where(low, tiles[a], rolled[a + 1]) for a in (0, 2)]
    odd = [jnp.where(low, rolled[a], tiles[a + 1]) for a in (0, 2)]
    return jnp.concatenate(even, 0), jnp.concatenate(odd, 0)


def body(
    n_lat, n_lon, scale, x_hbm, wc_hbm, wp_hbm, cot_hbm,
    enc_hbm, gin_hbm, gconv_ref, gpoint_ref,
    xb, x32, wc, wp, cot, halo_w, halo_e, chalo_w, chalo_e, c32,
    wd, pt, pe, preact, agrad, act, pre, pre_t, cot_t, pre32, pm, pp, enc, gout,
    sums, csend, crecv, msend, mrecv,
    x_sem, in_sem, out_sem, gout_sem, halo_send, halo_recv, c_sem_s, c_sem_r, m_sem_s, m_sem_r,
):
    lat, cols = x_hbm.shape[0], x_hbm.shape[1]
    out_cols = cols // 4
    main = lat * out_cols
    span = cols + 16
    pspan = out_cols + 16
    my_lat = lax.axis_index("lat")
    my_lon = lax.axis_index("lon")
    core = lax.rem(my_lat, 2)
    my_xhi = my_lat // 2
    chips = (n_lat // 2) * n_lon
    my_chip = my_xhi * n_lon + my_lon

    def peer(i):
        chip = lax.rem(my_chip + i, chips)
        return (chip // n_lon * 2 + core, lax.rem(chip, n_lon))

    partner = (my_xhi * 2 + 1 - core, my_lon)
    west = (my_lat, lax.rem(my_lon + n_lon - 1, n_lon))
    east = (my_lat, lax.rem(my_lon + 1, n_lon))

    barrier = pltpu.get_barrier_semaphore()

    def say(i, carry):
        pl.semaphore_signal(barrier, inc=1, device_id=peer(i), device_id_type=MESH)
        return carry

    lax.fori_loop(1, chips, say, 0)
    pl.semaphore_signal(barrier, inc=1, device_id=partner, device_id_type=MESH)

    wc_copy = pltpu.make_async_copy(wc_hbm, wc, in_sem.at[0])
    wp_copy = pltpu.make_async_copy(wp_hbm, wp, in_sem.at[1])
    cot_copy = pltpu.make_async_copy(cot_hbm, cot, in_sem.at[2])

    def x_copy(r):
        return pltpu.make_async_copy(x_hbm.at[r], xb.at[r], x_sem.at[r])

    wc_copy.start()
    for r in range(lat):
        x_copy(r).start()
    cot_copy.start()
    wp_copy.start()

    wc_copy.wait()
    lane_group = lax.broadcasted_iota(jnp.int32, (64, HALF), 1) // 64

    def spread(k, carry):
        for h in range(2):
            block = wc[pl.ds(pl.multiple_of(k * 64, 64), 64), h * HALF : (h + 1) * HALF].astype(F32)
            for g in range(4):
                at = pl.ds(pl.multiple_of(k * HALF + g * 64, 64), 64)
                wd[h, at, :] = jnp.where(lane_group == g, block, 0.0).astype(BF16)
        return carry

    lax.fori_loop(0, KW, spread, 0)

    def tap_lanes(k, l):
        start = k * HALF + (l % 2) * 128
        return slice(start, start + 128)

    def widen(r, carry):
        x_copy(r).wait()
        base = r * span
        zero = jnp.zeros((8, 128), F32)
        at = pl.ds(pl.multiple_of(r * out_cols, 16), out_cols)
        for l in range(4):
            x32[l, pl.ds(pl.multiple_of(base, 8), 8), :] = zero
            x32[l, pl.ds(pl.multiple_of(base + 8 + cols, 8), 8), :] = zero
            for s in range(0, cols, 16):
                x32[l, pl.ds(pl.multiple_of(base + 8 + s, 8), 16), :] = xb[
                    r, s : s + 16, l * 128 : (l + 1) * 128
                ].astype(F32)
        for k in range(KW):
            for l in range(4):
                taken = x32[l, pl.ds(base + 6 + k, out_cols, stride=4), :].astype(BF16)
                pt[l // 2, at, tap_lanes(k, l)] = taken
        return carry

    lax.fori_loop(0, lat, widen, 0)

    pl.semaphore_wait(barrier, chips)

    def remote(src, dst, to, s, r):
        return pltpu.make_async_remote_copy(
            src_ref=src, dst_ref=dst, send_sem=s, recv_sem=r, device_id=to, device_id_type=MESH
        )

    halos = [
        remote(x_hbm.at[:, 0:8, :], halo_e, west, halo_send.at[0], halo_recv.at[0]),
        remote(x_hbm.at[:, cols - 8 : cols, :], halo_w, east, halo_send.at[1], halo_recv.at[1]),
        remote(cot_hbm.at[:, 0:8, :], chalo_e, west, halo_send.at[2], halo_recv.at[2]),
        remote(cot_hbm.at[:, out_cols - 8 : out_cols, :], chalo_w, east, halo_send.at[3], halo_recv.at[3]),
    ]
    for h in halos:
        h.start()

    cot_copy.wait()
    wp_copy.wait()
    cot2 = cot[...].reshape(main, C)
    cot_t[...] = cot2.T
    agrad[0:main, :] = nt_dot(cot2, wp[...])

    step = main // 2

    def forward(c, carry):
        at = pl.ds(pl.multiple_of(c * step, 16), step)
        for h in range(2):
            y = dot(pt[h, at, :], wd[h])
            for i in range(2):
                preact[2 * h + i, at, :] = y[:, i * 128 : (i + 1) * 128]
        return carry

    lax.fori_loop(0, 2, forward, 0)

    for h in halos:
        h.wait()
    for r in range(lat):
        for l in range(4):
            lanes = slice(l * 128, (l + 1) * 128)
            x32[l, r * span : r * span + 8, :] = halo_w[r, :, lanes].astype(F32)
            x32[l, r * span + 8 + cols : r * span + 16 + cols, :] = halo_e[r, :, lanes].astype(F32)
            c32[l, r * 8 : r * 8 + 8, :] = chalo_w[r, :, lanes].astype(F32)
            c32[l, (lat + r) * 8 : (lat + r) * 8 + 8, :] = chalo_e[r, :, lanes].astype(F32)
    for r in range(lat):
        for k, j in ((0, 0), (1, 0), (6, out_cols - 16), (7, out_cols - 16)):
            for l in range(4):
                taken = x32[l, pl.ds(r * span + 6 + k + 4 * j, 16, stride=4), :].astype(BF16)
                pt[l // 2, r * out_cols + j : r * out_cols + j + 16, tap_lanes(k, l)] = taken
    for k in range(KW):
        for l in range(4):
            rows = [
                x32[l, pl.ds(4 * j + 6 + k, lat, stride=span), :]
                for j in (-1, out_cols, 0, out_cols - 1)
            ]
            pe[l // 2, :, tap_lanes(k, l)] = jnp.concatenate(rows, 0).astype(BF16)
    for h in range(2):
        edge = dot(pe[h], wd[h])
        for i in range(2):
            part = edge[:, i * 128 : (i + 1) * 128]
            preact[2 * h + i, main : main + 16, :] = part[0:16]
            preact[2 * h + i, pl.ds(0, lat, stride=out_cols), :] = part[16:24]
            preact[2 * h + i, pl.ds(out_cols - 1, lat, stride=out_cols), :] = part[24:32]
    cot_edge = jnp.concatenate(
        [
            jnp.concatenate(
                [c32[l, pl.ds(7, lat, stride=8), :], c32[l, pl.ds(lat * 8, lat, stride=8), :]], 0
            )
            for l in range(4)
        ],
        1,
    ).astype(BF16)
    agrad[main : main + 16, :] = nt_dot(cot_edge, wp[...])

    def gelu(at, l):
        z = preact[l, at, :]
        z2 = z * z
        th = jnp.tanh(GELU_C * (z + GELU_A * (z2 * z)))
        cdf = 0.5 * (1.0 + th)
        slope = cdf + (0.5 * z) * (1.0 - th * th) * (GELU_C * (1.0 + 3.0 * GELU_A * z2))
        return z * cdf, (agrad[at, l * 128 : (l + 1) * 128] * slope).astype(BF16)

    tiles = out_cols // 16

    def activate(r, carry):
        for t in range(tiles):
            at = pl.ds(pl.multiple_of(r * out_cols + t * 16, 16), 16)
            for l in range(4):
                lanes = slice(l * 128, (l + 1) * 128)
                a, p = gelu(at, l)
                act[at, lanes] = a.astype(BF16)
                pre[at, lanes] = p
                pre32[l, pl.ds(pl.multiple_of(r * pspan + 8 + t * 16, 8), 16), :] = p.astype(F32)
        return carry

    lax.fori_loop(0, lat, activate, 0)
    for l in range(4):
        edge_pre = gelu(slice(main, main + 16), l)[1].astype(F32)
        pre32[l, pl.ds(7, lat, stride=pspan), :] = edge_pre[0:8]
        pre32[l, pl.ds(8 + out_cols, lat, stride=pspan), :] = edge_pre[8:16]

    def core_rows(q, i):
        return pl.ds(pl.multiple_of((i // 16) * HALF + q * 128 + lax.rem(i, 16) * 8, 8), 8)

    def send_half(which):
        def one(i, carry):
            even, odd = messages(sums[which, core_rows(1 - core, i), :])
            csend[which, 2 * i] = even.astype(BF16)
            csend[which, 2 * i + 1] = odd.astype(BF16)
            return carry

        lax.fori_loop(0, 32, one, 0)
        pair(which).start()

    def pair(which):
        return remote(csend.at[which], crecv.at[which], partner, c_sem_s.at[which], c_sem_r.at[which])

    def send_all(which):
        pair(which).wait()

        def one(i, carry):
            even, odd = messages(sums[which, core_rows(core, i), :])
            msend[which, 2 * i] = (even + crecv[which, 2 * i].astype(F32)).astype(BF16)
            msend[which, 2 * i + 1] = (odd + crecv[which, 2 * i + 1].astype(F32)).astype(BF16)
            return carry

        lax.fori_loop(0, 32, one, 0)

        def push(i, carry):
            chip = lax.rem(my_chip + i, chips)
            remote(
                msend.at[which, chip], mrecv.at[which, i - 1], peer(i), m_sem_s.at[which], m_sem_r.at[which]
            ).start()
            return carry

        lax.fori_loop(1, chips, push, 0)

    def collect(which, out_ref):
        everything = pltpu.make_async_copy(
            msend.at[which, 0 : chips - 1], mrecv.at[which], m_sem_r.at[which]
        )
        everything.wait()
        pltpu.make_async_copy(
            msend.at[which, 0 : chips - 1], mrecv.at[which], m_sem_s.at[which]
        ).wait()

        def one(i, carry):
            return carry + mrecv[which, i].astype(F32)

        total = lax.fori_loop(0, chips - 1, one, msend[which, my_chip].astype(F32), unroll=7)
        out_ref[...] = total * scale

    for c in range(2):
        rows = slice(c * HALF, (c + 1) * HALF)
        sums[0, rows, :] = dot(cot_t[rows, :], act[...])
    send_half(0)

    enc[...] = dot(act[...], wp[...]).astype(BF16).reshape(lat, out_cols, C)
    enc_copy = pltpu.make_async_copy(enc, enc_hbm, out_sem.at[0])
    enc_copy.start()
    pre_t[...] = pre[...].T
    send_all(0)

    low_lanes = lax.broadcasted_iota(jnp.int32, (64, 128), 1) < 64

    def conv_grad(p, carry):
        for h in range(2):
            lanes = pl.ds(pl.multiple_of(p * 2 * HALF, 2 * HALF), 2 * HALF)
            both = dot(pre_t[h * HALF : (h + 1) * HALF, :], pt[h, 0:main, lanes])
            for g in range(4):
                rows = slice(g * 64, g * 64 + 64)
                tile = (g // 2) * 128
                a = both[rows, tile : tile + 128]
                b = both[rows, HALF + tile : HALF + tile + 128]
                if g % 2 == 0:
                    b = pltpu.roll(b, 64, 1)
                else:
                    a = pltpu.roll(a, 64, 1)
                sums[1, h * HALF + g * 64 : h * HALF + g * 64 + 64, pl.ds(pl.multiple_of(p * 128, 128), 128)] = (
                    jnp.where(low_lanes, a, b)
                )
        return carry

    lax.fori_loop(0, KW // 2, conv_grad, 0)
    send_half(1)

    for r in range(lat):
        at = slice(r * out_cols, (r + 1) * out_cols)
        for l in range(4):
            lanes = slice(l * 128, (l + 1) * 128)
            pm[at, lanes] = pre32[l, r * pspan + 7 : r * pspan + 7 + out_cols, :].astype(BF16)
            pp[at, lanes] = pre32[l, r * pspan + 9 : r * pspan + 9 + out_cols, :].astype(BF16)
    send_all(1)

    gblock = 4

    def gout_copy(c):
        return pltpu.make_async_copy(
            gout.at[pl.ds(c * gblock, gblock)], gin_hbm.at[pl.ds(c * gblock, gblock)], gout_sem.at[c]
        )

    def input_grad(c, carry):
        rows = gblock * out_cols
        at = pl.ds(pl.multiple_of(c * rows, 16), rows)
        for h in range(2):
            lanes = slice(h * HALF, (h + 1) * HALF)
            here = pre[at, lanes]
            for m, (first, second, shifted) in enumerate(((2, 6, pm), (3, 7, pm), (4, 0, pp), (5, 1, pp))):
                y = nt_dot(here, wd[h, first * HALF : (first + 1) * HALF, :]) + nt_dot(
                    shifted[at, lanes], wd[h, second * HALF : (second + 1) * HALF, :]
                )
                for r in range(gblock):
                    for i in range(2):
                        x32[2 * h + i, pl.ds((c * gblock + r) * cols + m, out_cols, stride=4), :] = y[
                            r * out_cols : (r + 1) * out_cols, i * 128 : (i + 1) * 128
                        ]
        for r in range(gblock):
            row = c * gblock + r
            for s in range(0, cols, 16):
                for l in range(4):
                    gout[row, s : s + 16, l * 128 : (l + 1) * 128] = x32[
                        l, pl.ds(pl.multiple_of(row * cols + s, 16), 16), :
                    ].astype(BF16)
        gout_copy(c).start()
        return carry

    lax.fori_loop(0, lat // gblock, input_grad, 0)

    collect(0, gpoint_ref)
    collect(1, gconv_ref)
    enc_copy.wait()
    for c in range(lat // gblock):
        gout_copy(c).wait()


def per_device(n_lat, n_lon, inputs, w_conv, w_point, cotangent):
    lat, cols, channels = inputs.shape
    out_cols = cols // 4
    main = lat * out_cols
    chips = (n_lat // 2) * n_lon
    scale = 1.0 / math.sqrt(main * n_lat * n_lon)
    dma = pltpu.SemaphoreType.DMA
    scratch = [
        pltpu.VMEM((lat, cols, C), BF16),
        pltpu.VMEM((4, lat * (cols + 16), 128), F32),
        pltpu.VMEM((C, C), BF16),
        pltpu.VMEM((C, C), BF16),
        pltpu.VMEM((lat, out_cols, C), BF16),
        pltpu.VMEM((lat, 8, C), BF16),
        pltpu.VMEM((lat, 8, C), BF16),
        pltpu.VMEM((lat, 8, C), BF16),
        pltpu.VMEM((lat, 8, C), BF16),
        pltpu.VMEM((4, 2 * lat * 8, 128), F32),
        pltpu.VMEM((2, KW * HALF, HALF), BF16),
        pltpu.VMEM((2, main, KW * HALF), BF16),
        pltpu.VMEM((2, 32, KW * HALF), BF16),
        pltpu.VMEM((4, main + 16, 128), F32),
        pltpu.VMEM((main + 16, C), F32),
        pltpu.VMEM((main, C), BF16),
        pltpu.VMEM((main, C), BF16),
        pltpu.VMEM((C, main), BF16),
        pltpu.VMEM((C, main), BF16),
        pltpu.VMEM((4, lat * (out_cols + 16), 128), F32),
        pltpu.VMEM((main, C), BF16),
        pltpu.VMEM((main, C), BF16),
        pltpu.VMEM((lat, out_cols, C), BF16),
        pltpu.VMEM((lat, cols, C), BF16),
        pltpu.VMEM((2, C, C), F32),
        pltpu.VMEM((2, chips, 16, 128), BF16),
        pltpu.VMEM((2, chips, 16, 128), BF16),
        pltpu.VMEM((2, chips, 16, 128), BF16),
        pltpu.VMEM((2, chips - 1, 16, 128), BF16),
        dma((lat,)),
        dma((3,)),
        dma((1,)),
        dma((2,)),
        dma((4,)),
        dma((4,)),
        dma((2,)),
        dma((2,)),
        dma((2,)),
        dma((2,)),
    ]
    any_spec = pl.BlockSpec(memory_space=pl.ANY)
    vmem_spec = pl.BlockSpec(memory_space=pltpu.VMEM)
    encoded, grad_inputs, conv, point = pl.pallas_call(
        functools.partial(body, n_lat, n_lon, scale),
        out_shape=(
            jax.ShapeDtypeStruct((lat, out_cols, C), BF16),
            jax.ShapeDtypeStruct((lat, cols, C), BF16),
            jax.ShapeDtypeStruct((16, 128), F32),
            jax.ShapeDtypeStruct((16, 128), F32),
        ),
        in_specs=[any_spec] * 4,
        out_specs=(any_spec, any_spec, vmem_spec, vmem_spec),
        scratch_shapes=scratch,
        compiler_params=pltpu.CompilerParams(
            collective_id=0, has_side_effects=True, vmem_limit_bytes=60 * 1024 * 1024
        ),
        name="conv_step",
    )(inputs, w_conv, w_point, cotangent)

    def unfold(block):
        return block.reshape(4, 4, 128).transpose(0, 2, 1).reshape(C, 4)

    return encoded, grad_inputs, unfold(conv), unfold(point)


def solution(mesh):
    placed = (P("lat", "lon", None), P(), P(), P("lat", "lon", None))
    return jax.shard_map(
        functools.partial(per_device, mesh.shape["lat"], mesh.shape["lon"]),
        mesh=mesh,
        in_specs=placed,
        out_specs=(
            P("lat", "lon", None),
            P("lat", "lon", None),
            P(None, ("lat", "lon")),
            P(None, ("lat", "lon")),
        ),
        check_vma=False,
    )
```

```python
import functools
import math

import jax
import jax.numpy as jnp
from jax import lax
from jax.experimental import pallas as pl
from jax.experimental.pallas import tpu as pltpu
from jax.sharding import PartitionSpec as P

MESH = pl.DeviceIdType.MESH
F32 = jnp.float32
BF16 = jnp.bfloat16
G = 8
KW = 8
C = 512
HALF = 256
GELU_C = math.sqrt(2.0 / math.pi)
GELU_A = 0.044715


def nt_dot(a, b):
    return lax.dot_general(a, b, (((1,), (1,)), ((), ())), preferred_element_type=F32)


def dot(a, b):
    return jnp.dot(a, b, preferred_element_type=F32)


def messages(rows8):
    low = lax.broadcasted_iota(jnp.int32, (8, 128), 0) < 4
    tiles = [rows8[:, l * 128 : (l + 1) * 128] for l in range(4)]
    rolled = [pltpu.roll(t, 4, 0) for t in tiles]
    even = [jnp.where(low, tiles[a], rolled[a + 1]) for a in (0, 2)]
    odd = [jnp.where(low, rolled[a], tiles[a + 1]) for a in (0, 2)]
    return jnp.concatenate(even, 0), jnp.concatenate(odd, 0)


def remote(src, dst, to, s, r):
    return pltpu.make_async_remote_copy(
        src_ref=src, dst_ref=dst, send_sem=s, recv_sem=r, device_id=to, device_id_type=MESH
    )


def open_body(
    n_lon, x_hbm, wc_hbm, wp_hbm, cot_hbm, pt, wd, preact, agrad, cot_t,
    xb, x32, wc, wp, cot, halo_w, halo_e, chalo_w, chalo_e, c32, pe,
    x_sem, in_sem, halo_send, halo_recv,
):
    lat, cols = x_hbm.shape[0], x_hbm.shape[1]
    out_cols = cols // 4
    main = lat * out_cols
    span = cols + 16
    my_lat = lax.axis_index("lat")
    my_lon = lax.axis_index("lon")
    west = (my_lat, lax.rem(my_lon + n_lon - 1, n_lon))
    east = (my_lat, lax.rem(my_lon + 1, n_lon))

    barrier = pltpu.get_barrier_semaphore()
    for side in (west, east):
        pl.semaphore_signal(barrier, inc=1, device_id=side, device_id_type=MESH)

    wc_copy = pltpu.make_async_copy(wc_hbm, wc, in_sem.at[0])
    wp_copy = pltpu.make_async_copy(wp_hbm, wp, in_sem.at[1])
    cot_copy = pltpu.make_async_copy(cot_hbm, cot, in_sem.at[2])

    def x_copy(r):
        return pltpu.make_async_copy(x_hbm.at[r], xb.at[r], x_sem.at[r])

    wc_copy.start()
    cot_copy.start()
    wp_copy.start()
    for r in range(lat):
        x_copy(r).start()

    pl.semaphore_wait(barrier, 2)
    halos = [
        remote(x_hbm.at[:, 0:8, :], halo_e, west, halo_send.at[0], halo_recv.at[0]),
        remote(x_hbm.at[:, cols - 8 : cols, :], halo_w, east, halo_send.at[1], halo_recv.at[1]),
        remote(cot_hbm.at[:, 0:8, :], chalo_e, west, halo_send.at[2], halo_recv.at[2]),
        remote(cot_hbm.at[:, out_cols - 8 : out_cols, :], chalo_w, east, halo_send.at[3], halo_recv.at[3]),
    ]
    for h in halos:
        h.start()

    wc_copy.wait()
    lane_group = lax.broadcasted_iota(jnp.int32, (64, HALF), 1) // 64

    def spread(k, carry):
        for h in range(2):
            block = wc[pl.ds(pl.multiple_of(k * 64, 64), 64), h * HALF : (h + 1) * HALF].astype(F32)
            for g in range(4):
                at = pl.ds(pl.multiple_of(k * HALF + g * 64, 64), 64)
                wd[h, at, :] = jnp.where(lane_group == g, block, 0.0).astype(BF16)
        return carry

    lax.fori_loop(0, KW, spread, 0)

    def tap_lanes(k, l):
        start = k * HALF + (l % 2) * 128
        return slice(start, start + 128)

    def widen(r, carry):
        x_copy(r).wait()
        base = r * span
        zero = jnp.zeros((8, 128), F32)
        at = pl.ds(pl.multiple_of(r * out_cols, 16), out_cols)
        for l in range(4):
            x32[l, pl.ds(pl.multiple_of(base, 8), 8), :] = zero
            x32[l, pl.ds(pl.multiple_of(base + 8 + cols, 8), 8), :] = zero
            for s in range(0, cols, 16):
                x32[l, pl.ds(pl.multiple_of(base + 8 + s, 8), 16), :] = xb[
                    r, s : s + 16, l * 128 : (l + 1) * 128
                ].astype(F32)
        for k in range(KW):
            for l in range(4):
                taken = x32[l, pl.ds(base + 6 + k, out_cols, stride=4), :].astype(BF16)
                pt[l // 2, at, tap_lanes(k, l)] = taken
        return carry

    lax.fori_loop(0, lat, widen, 0)

    cot_copy.wait()
    wp_copy.wait()
    cot2 = cot[...].reshape(main, C)
    cot_t[...] = cot2.T
    agrad[0:main, :] = nt_dot(cot2, wp[...])

    step = main // 2

    def forward(c, carry):
        at = pl.ds(pl.multiple_of(c * step, 16), step)
        for h in range(2):
            y = dot(pt[h, at, :], wd[h])
            for i in range(2):
                preact[2 * h + i, at, :] = y[:, i * 128 : (i + 1) * 128]
        return carry

    lax.fori_loop(0, 2, forward, 0)

    for h in halos:
        h.wait()
    for r in range(lat):
        for l in range(4):
            lanes = slice(l * 128, (l + 1) * 128)
            x32[l, r * span : r * span + 8, :] = halo_w[r, :, lanes].astype(F32)
            x32[l, r * span + 8 + cols : r * span + 16 + cols, :] = halo_e[r, :, lanes].astype(F32)
            c32[l, r * 8 : r * 8 + 8, :] = chalo_w[r, :, lanes].astype(F32)
            c32[l, (lat + r) * 8 : (lat + r) * 8 + 8, :] = chalo_e[r, :, lanes].astype(F32)
    for r in range(lat):
        for k, j in ((0, 0), (1, 0), (6, out_cols - 16), (7, out_cols - 16)):
            for l in range(4):
                taken = x32[l, pl.ds(r * span + 6 + k + 4 * j, 16, stride=4), :].astype(BF16)
                pt[l // 2, r * out_cols + j : r * out_cols + j + 16, tap_lanes(k, l)] = taken
    for k in range(KW):
        for l in range(4):
            rows = [
                x32[l, pl.ds(4 * j + 6 + k, lat, stride=span), :]
                for j in (-1, out_cols, 0, out_cols - 1)
            ]
            pe[l // 2, :, tap_lanes(k, l)] = jnp.concatenate(rows, 0).astype(BF16)
    for h in range(2):
        edge = dot(pe[h], wd[h])
        for i in range(2):
            part = edge[:, i * 128 : (i + 1) * 128]
            preact[2 * h + i, main : main + 16, :] = part[0:16]
            preact[2 * h + i, pl.ds(0, lat, stride=out_cols), :] = part[16:24]
            preact[2 * h + i, pl.ds(out_cols - 1, lat, stride=out_cols), :] = part[24:32]
    cot_edge = jnp.concatenate(
        [
            jnp.concatenate(
                [c32[l, pl.ds(7, lat, stride=8), :], c32[l, pl.ds(lat * 8, lat, stride=8), :]], 0
            )
            for l in range(4)
        ],
        1,
    ).astype(BF16)
    agrad[main : main + 16, :] = nt_dot(cot_edge, wp[...])


def close_body(
    n_lat, n_lon, scale, lat, cols, wp_hbm, pt, wd, preact, agrad, cot_t,
    enc, gout, gconv_ref, gpoint_ref,
    wp, act, pre, pre_t, pre32, pm, pp, g32, sums, csend, crecv, msend, mrecv,
    in_sem, c_sem_s, c_sem_r, m_sem_s, m_sem_r,
):
    out_cols = cols // 4
    main = lat * out_cols
    pspan = out_cols + 16
    my_lat = lax.axis_index("lat")
    my_lon = lax.axis_index("lon")
    core = lax.rem(my_lat, 2)
    my_xhi = my_lat // 2
    chips = (n_lat // 2) * n_lon
    my_chip = my_xhi * n_lon + my_lon

    def peer(i):
        chip = lax.rem(my_chip + i, chips)
        return (chip // n_lon * 2 + core, lax.rem(chip, n_lon))

    partner = (my_xhi * 2 + 1 - core, my_lon)
    barrier = pltpu.get_barrier_semaphore()

    def say(i, carry):
        pl.semaphore_signal(barrier, inc=1, device_id=peer(i), device_id_type=MESH)
        return carry

    lax.fori_loop(1, chips, say, 0, unroll=9)
    pl.semaphore_signal(barrier, inc=1, device_id=partner, device_id_type=MESH)
    wp_copy = pltpu.make_async_copy(wp_hbm, wp, in_sem.at[0])
    wp_copy.start()

    def gelu(at, l):
        z = preact[l, at, :]
        z2 = z * z
        th = jnp.tanh(GELU_C * (z + GELU_A * (z2 * z)))
        cdf = 0.5 * (1.0 + th)
        slope = cdf + (0.5 * z) * (1.0 - th * th) * (GELU_C * (1.0 + 3.0 * GELU_A * z2))
        return z * cdf, (agrad[at, l * 128 : (l + 1) * 128] * slope).astype(BF16)

    tiles = out_cols // 16

    def activate(r, carry):
        for t in range(tiles):
            at = pl.ds(pl.multiple_of(r * out_cols + t * 16, 16), 16)
            for l in range(4):
                lanes = slice(l * 128, (l + 1) * 128)
                a, p = gelu(at, l)
                act[at, lanes] = a.astype(BF16)
                pre[at, lanes] = p
                pre32[l, pl.ds(pl.multiple_of(r * pspan + 8 + t * 16, 8), 16), :] = p.astype(F32)
        return carry

    lax.fori_loop(0, lat, activate, 0)
    for l in range(4):
        edge_pre = gelu(slice(main, main + 16), l)[1].astype(F32)
        pre32[l, pl.ds(7, lat, stride=pspan), :] = edge_pre[0:8]
        pre32[l, pl.ds(8 + out_cols, lat, stride=pspan), :] = edge_pre[8:16]

    def core_rows(q, i):
        return pl.ds(pl.multiple_of((i // 16) * HALF + q * 128 + lax.rem(i, 16) * 8, 8), 8)

    def send_half(which):
        def one(i, carry):
            even, odd = messages(sums[which, core_rows(1 - core, i), :])
            csend[which, 2 * i] = even.astype(BF16)
            csend[which, 2 * i + 1] = odd.astype(BF16)
            return carry

        lax.fori_loop(0, 32, one, 0, unroll=4)

    def pair(which):
        return remote(csend.at[which], crecv.at[which], partner, c_sem_s.at[which], c_sem_r.at[which])

    def send_all(which):
        pair(which).wait()

        def one(i, carry):
            even, odd = messages(sums[which, core_rows(core, i), :])
            msend[which, 2 * i] = (even + crecv[which, 2 * i].astype(F32)).astype(BF16)
            msend[which, 2 * i + 1] = (odd + crecv[which, 2 * i + 1].astype(F32)).astype(BF16)
            return carry

        lax.fori_loop(0, 32, one, 0, unroll=4)

        def push(i, carry):
            chip = lax.rem(my_chip + i, chips)
            remote(
                msend.at[which, chip], mrecv.at[which, i - 1], peer(i), m_sem_s.at[which], m_sem_r.at[which]
            ).start()
            return carry

        lax.fori_loop(1, chips, push, 0, unroll=9)

    def collect(which, out_ref):
        everything = pltpu.make_async_copy(
            msend.at[which, 0 : chips - 1], mrecv.at[which], m_sem_r.at[which]
        )
        everything.wait()
        pltpu.make_async_copy(
            msend.at[which, 0 : chips - 1], mrecv.at[which], m_sem_s.at[which]
        ).wait()

        def one(i, carry):
            return carry + mrecv[which, i].astype(F32)

        total = lax.fori_loop(0, chips - 1, one, msend[which, my_chip].astype(F32), unroll=7)
        out_ref[...] = total * scale

    for c in range(2):
        rows = slice(c * HALF, (c + 1) * HALF)
        sums[0, rows, :] = dot(cot_t[rows, :], act[...])
    send_half(0)
    pre_t[...] = pre[...].T

    low_lanes = lax.broadcasted_iota(jnp.int32, (64, 128), 1) < 64

    def conv_grad(p, carry):
        for h in range(2):
            lanes = pl.ds(pl.multiple_of(p * 2 * HALF, 2 * HALF), 2 * HALF)
            both = dot(pre_t[h * HALF : (h + 1) * HALF, :], pt[h, 0:main, lanes])
            for g in range(4):
                rows = slice(g * 64, g * 64 + 64)
                tile = (g // 2) * 128
                a = both[rows, tile : tile + 128]
                b = both[rows, HALF + tile : HALF + tile + 128]
                if g % 2 == 0:
                    b = pltpu.roll(b, 64, 1)
                else:
                    a = pltpu.roll(a, 64, 1)
                sums[1, h * HALF + g * 64 : h * HALF + g * 64 + 64, pl.ds(pl.multiple_of(p * 128, 128), 128)] = (
                    jnp.where(low_lanes, a, b)
                )
        return carry

    lax.fori_loop(0, KW // 2, conv_grad, 0)
    send_half(1)
    pl.semaphore_wait(barrier, chips)
    pair(0).start()
    pair(1).start()

    wp_copy.wait()
    enc[...] = dot(act[...], wp[...]).astype(BF16).reshape(lat, out_cols, C)
    send_all(0)
    send_all(1)

    for r in range(lat):
        at = slice(r * out_cols, (r + 1) * out_cols)
        for l in range(4):
            lanes = slice(l * 128, (l + 1) * 128)
            pm[at, lanes] = pre32[l, r * pspan + 7 : r * pspan + 7 + out_cols, :].astype(BF16)
            pp[at, lanes] = pre32[l, r * pspan + 9 : r * pspan + 9 + out_cols, :].astype(BF16)

    gblock = 4

    def input_grad(c, carry):
        rows = gblock * out_cols
        at = pl.ds(pl.multiple_of(c * rows, 16), rows)
        for h in range(2):
            lanes = slice(h * HALF, (h + 1) * HALF)
            here = pre[at, lanes]
            for m, (first, second, shifted) in enumerate(((2, 6, pm), (3, 7, pm), (4, 0, pp), (5, 1, pp))):
                y = nt_dot(here, wd[h, first * HALF : (first + 1) * HALF, :]) + nt_dot(
                    shifted[at, lanes], wd[h, second * HALF : (second + 1) * HALF, :]
                )
                for r in range(gblock):
                    for i in range(2):
                        g32[2 * h + i, pl.ds((c * gblock + r) * cols + m, out_cols, stride=4), :] = y[
                            r * out_cols : (r + 1) * out_cols, i * 128 : (i + 1) * 128
                        ]
        for r in range(gblock):
            row = c * gblock + r
            for s in range(0, cols, 16):
                for l in range(4):
                    gout[row, s : s + 16, l * 128 : (l + 1) * 128] = g32[
                        l, pl.ds(pl.multiple_of(row * cols + s, 16), 16), :
                    ].astype(BF16)
        return carry

    lax.fori_loop(0, lat // gblock, input_grad, 0)

    collect(0, gpoint_ref)
    collect(1, gconv_ref)


def drain_body(enc, gout, conv, point, enc_hbm, gin_hbm, conv_hbm, point_hbm, sems):
    moves = [
        pltpu.make_async_copy(src, dst, sems.at[i])
        for i, (src, dst) in enumerate(
            ((gout, gin_hbm), (enc, enc_hbm), (conv, conv_hbm), (point, point_hbm))
        )
    ]
    for m in moves:
        m.start()
    for m in moves:
        m.wait()


def per_device(n_lat, n_lon, inputs, w_conv, w_point, cotangent):
    lat, cols, channels = inputs.shape
    out_cols = cols // 4
    main = lat * out_cols
    chips = (n_lat // 2) * n_lon
    scale = 1.0 / math.sqrt(main * n_lat * n_lon)
    dma = pltpu.SemaphoreType.DMA
    vmem = pltpu.VMEM
    any_spec = pl.BlockSpec(memory_space=pl.ANY)
    vmem_spec = pl.BlockSpec(memory_space=pltpu.VMEM)

    handed = pl.pallas_call(
        functools.partial(open_body, n_lon),
        out_shape=(
            vmem((2, main, KW * HALF), BF16),
            vmem((2, KW * HALF, HALF), BF16),
            vmem((4, main + 16, 128), F32),
            vmem((main + 16, C), F32),
            vmem((C, main), BF16),
        ),
        in_specs=[any_spec] * 4,
        out_specs=(vmem_spec,) * 5,
        scratch_shapes=[
            vmem((lat, cols, C), BF16),
            vmem((4, lat * (cols + 16), 128), F32),
            vmem((C, C), BF16),
            vmem((C, C), BF16),
            vmem((lat, out_cols, C), BF16),
            vmem((lat, 8, C), BF16),
            vmem((lat, 8, C), BF16),
            vmem((lat, 8, C), BF16),
            vmem((lat, 8, C), BF16),
            vmem((4, 2 * lat * 8, 128), F32),
            vmem((2, 32, KW * HALF), BF16),
            dma((lat,)),
            dma((3,)),
            dma((4,)),
            dma((4,)),
        ],
        compiler_params=pltpu.CompilerParams(
            collective_id=1, has_side_effects=True, vmem_limit_bytes=32 * 1024 * 1024
        ),
        name="forward_step",
    )(inputs, w_conv, w_point, cotangent)

    results = pl.pallas_call(
        functools.partial(close_body, n_lat, n_lon, scale, lat, cols),
        out_shape=(
            vmem((lat, out_cols, C), BF16),
            vmem((lat, cols, C), BF16),
            vmem((16, 128), F32),
            vmem((16, 128), F32),
        ),
        in_specs=[any_spec] + [vmem_spec] * 5,
        out_specs=(vmem_spec,) * 4,
        scratch_shapes=[
            vmem((C, C), BF16),
            vmem((main, C), BF16),
            vmem((main, C), BF16),
            vmem((C, main), BF16),
            vmem((4, lat * (out_cols + 16), 128), F32),
            vmem((main, C), BF16),
            vmem((main, C), BF16),
            vmem((4, lat * cols, 128), F32),
            vmem((2, C, C), F32),
            vmem((2, chips, 16, 128), BF16),
            vmem((2, chips, 16, 128), BF16),
            vmem((2, chips, 16, 128), BF16),
            vmem((2, chips - 1, 16, 128), BF16),
            dma((1,)),
            dma((2,)),
            dma((2,)),
            dma((2,)),
            dma((2,)),
        ],
        compiler_params=pltpu.CompilerParams(
            collective_id=0, has_side_effects=True, vmem_limit_bytes=40 * 1024 * 1024
        ),
        name="backward_step",
    )(w_point, *handed)

    encoded, grad_inputs, conv, point = pl.pallas_call(
        drain_body,
        out_shape=(
            jax.ShapeDtypeStruct((lat, out_cols, C), BF16),
            jax.ShapeDtypeStruct((lat, cols, C), BF16),
            jax.ShapeDtypeStruct((16, 128), F32),
            jax.ShapeDtypeStruct((16, 128), F32),
        ),
        in_specs=[vmem_spec] * 4,
        out_specs=(any_spec,) * 4,
        scratch_shapes=[dma((4,))],
        name="drain",
    )(*results)

    def unfold(block):
        return block.reshape(4, 4, 128).transpose(0, 2, 1).reshape(C, 4)

    return encoded, grad_inputs, unfold(conv), unfold(point)


def solution(mesh):
    placed = (P("lat", "lon", None), P(), P(), P("lat", "lon", None))
    return jax.shard_map(
        functools.partial(per_device, mesh.shape["lat"], mesh.shape["lon"]),
        mesh=mesh,
        in_specs=placed,
        out_specs=(
            P("lat", "lon", None),
            P("lat", "lon", None),
            P(None, ("lat", "lon")),
            P(None, ("lat", "lon")),
        ),
        check_vma=False,
    )
```

```python
import functools
import math

import jax
import jax.numpy as jnp
from jax import lax
from jax.experimental import pallas as pl
from jax.experimental.pallas import tpu as pltpu
from jax.sharding import PartitionSpec as P

MESH = pl.DeviceIdType.MESH
F32 = jnp.float32
BF16 = jnp.bfloat16
G = 8
KW = 8
C = 512
HALF = 256
GELU_C = math.sqrt(2.0 / math.pi)
GELU_A = 0.044715


def nt_dot(a, b):
    return lax.dot_general(a, b, (((1,), (1,)), ((), ())), preferred_element_type=F32)


def dot(a, b):
    return jnp.dot(a, b, preferred_element_type=F32)


def messages(tiles):
    low = lax.broadcasted_iota(jnp.int32, (8, 128), 0) < 4
    rolled = [pltpu.roll(t, 4, 0) for t in tiles]
    even = [jnp.where(low, tiles[a], rolled[a + 1]) for a in (0, 2)]
    odd = [jnp.where(low, rolled[a], tiles[a + 1]) for a in (0, 2)]
    return jnp.concatenate(even, 0), jnp.concatenate(odd, 0)


def remote(src, dst, to, s, r):
    return pltpu.make_async_remote_copy(
        src_ref=src, dst_ref=dst, send_sem=s, recv_sem=r, device_id=to, device_id_type=MESH
    )


def open_body(
    n_lon, x_hbm, wc_hbm, cot_hbm, pt, wd, cot_edge,
    xb, x32, wc, halo_w, halo_e, chalo_w, chalo_e, c32,
    x_sem, in_sem, halo_send, halo_recv,
):
    lat, cols = x_hbm.shape[0], x_hbm.shape[1]
    out_cols = cols // 4
    main = lat * out_cols
    span = cols + 16
    my_lat = lax.axis_index("lat")
    my_lon = lax.axis_index("lon")
    west = (my_lat, lax.rem(my_lon + n_lon - 1, n_lon))
    east = (my_lat, lax.rem(my_lon + 1, n_lon))

    barrier = pltpu.get_barrier_semaphore()
    for side in (west, east):
        pl.semaphore_signal(barrier, inc=1, device_id=side, device_id_type=MESH)

    wc_copy = pltpu.make_async_copy(wc_hbm, wc, in_sem.at[0])

    def x_copy(r):
        return pltpu.make_async_copy(x_hbm.at[r], xb.at[r], x_sem.at[r])

    wc_copy.start()
    for r in range(lat):
        x_copy(r).start()

    pl.semaphore_wait(barrier, 2)
    halos = [
        remote(x_hbm.at[:, 0:8, :], halo_e, west, halo_send.at[0], halo_recv.at[0]),
        remote(x_hbm.at[:, cols - 8 : cols, :], halo_w, east, halo_send.at[1], halo_recv.at[1]),
        remote(cot_hbm.at[:, 0:8, :], chalo_e, west, halo_send.at[2], halo_recv.at[2]),
        remote(cot_hbm.at[:, out_cols - 8 : out_cols, :], chalo_w, east, halo_send.at[3], halo_recv.at[3]),
    ]
    for h in halos:
        h.start()

    wc_copy.wait()
    lane_group = lax.broadcasted_iota(jnp.int32, (64, HALF), 1) // 64

    def spread(k, carry):
        for h in range(2):
            block = wc[pl.ds(pl.multiple_of(k * 64, 64), 64), h * HALF : (h + 1) * HALF].astype(F32)
            for g in range(4):
                at = pl.ds(pl.multiple_of(k * HALF + g * 64, 64), 64)
                wd[h, at, :] = jnp.where(lane_group == g, block, 0.0).astype(BF16)
        return carry

    lax.fori_loop(0, KW, spread, 0)

    def tap_lanes(k, l):
        start = k * HALF + (l % 2) * 128
        return slice(start, start + 128)

    def widen(r, carry):
        x_copy(r).wait()
        base = r * span
        zero = jnp.zeros((8, 128), F32)
        at = pl.ds(pl.multiple_of(r * out_cols, 16), out_cols)
        for l in range(4):
            x32[l, pl.ds(pl.multiple_of(base, 8), 8), :] = zero
            x32[l, pl.ds(pl.multiple_of(base + 8 + cols, 8), 8), :] = zero
            for s in range(0, cols, 16):
                x32[l, pl.ds(pl.multiple_of(base + 8 + s, 8), 16), :] = xb[
                    r, s : s + 16, l * 128 : (l + 1) * 128
                ].astype(F32)
        for k in range(KW):
            for l in range(4):
                taken = x32[l, pl.ds(base + 6 + k, out_cols, stride=4), :].astype(BF16)
                pt[l // 2, at, tap_lanes(k, l)] = taken
        return carry

    lax.fori_loop(0, lat, widen, 0)

    for h in halos:
        h.wait()
    for r in range(lat):
        for l in range(4):
            lanes = slice(l * 128, (l + 1) * 128)
            x32[l, r * span : r * span + 8, :] = halo_w[r, :, lanes].astype(F32)
            x32[l, r * span + 8 + cols : r * span + 16 + cols, :] = halo_e[r, :, lanes].astype(F32)
            c32[l, r * 8 : r * 8 + 8, :] = chalo_w[r, :, lanes].astype(F32)
            c32[l, (lat + r) * 8 : (lat + r) * 8 + 8, :] = chalo_e[r, :, lanes].astype(F32)
    for r in range(lat):
        for k, j in ((0, 0), (1, 0), (6, out_cols - 16), (7, out_cols - 16)):
            for l in range(4):
                taken = x32[l, pl.ds(r * span + 6 + k + 4 * j, 16, stride=4), :].astype(BF16)
                pt[l // 2, r * out_cols + j : r * out_cols + j + 16, tap_lanes(k, l)] = taken
    for k in range(KW):
        for l in range(4):
            rows = [x32[l, pl.ds(4 * j + 6 + k, lat, stride=span), :] for j in (-1, out_cols)]
            pt[l // 2, main : main + 16, tap_lanes(k, l)] = jnp.concatenate(rows, 0).astype(BF16)
    for l in range(4):
        rows = [c32[l, pl.ds(7, lat, stride=8), :], c32[l, pl.ds(lat * 8, lat, stride=8), :]]
        cot_edge[:, l * 128 : (l + 1) * 128] = jnp.concatenate(rows, 0).astype(BF16)


def close_body(
    n_lat, n_lon, scale, lat, cols, wp_hbm, cot_hbm, pt, wd, cot_edge,
    enc, gout, gconv_ref, gpoint_ref,
    wp, cot, preact, agrad, cot_t, act, pre, pre_t, pre32, pm, pp, g32, sums, crecv, msend, mrecv,
    in_sem, c_sem_s, c_sem_r, m_sem_s, m_sem_r,
):
    out_cols = cols // 4
    main = lat * out_cols
    pspan = out_cols + 16
    my_lat = lax.axis_index("lat")
    my_lon = lax.axis_index("lon")
    core = lax.rem(my_lat, 2)
    my_xhi = my_lat // 2
    chips = (n_lat // 2) * n_lon
    my_chip = my_xhi * n_lon + my_lon

    def peer(i):
        chip = lax.rem(my_chip + i, chips)
        return (chip // n_lon * 2 + core, lax.rem(chip, n_lon))

    partner = (my_xhi * 2 + 1 - core, my_lon)
    barrier = pltpu.get_barrier_semaphore()

    def say(i, carry):
        pl.semaphore_signal(barrier, inc=1, device_id=peer(i), device_id_type=MESH)
        return carry

    lax.fori_loop(1, chips, say, 0, unroll=9)
    pl.semaphore_signal(barrier, inc=1, device_id=partner, device_id_type=MESH)
    wp_copy = pltpu.make_async_copy(wp_hbm, wp, in_sem.at[0])
    cot_copy = pltpu.make_async_copy(cot_hbm, cot, in_sem.at[1])
    wp_copy.start()
    cot_copy.start()

    def forward(rows):
        for h in range(2):
            y = dot(pt[h, rows, :], wd[h])
            for i in range(2):
                preact[2 * h + i, rows, :] = y[:, i * 128 : (i + 1) * 128]

    step = main // 2

    def forward_part(c, carry):
        forward(pl.ds(pl.multiple_of(c * step, 16), step))
        return carry

    lax.fori_loop(0, 2, forward_part, 0)
    forward(slice(main, main + 16))
    wp_copy.wait()
    cot_copy.wait()
    cot2 = cot[...].reshape(main, C)
    cot_t[...] = cot2.T
    agrad[0:main, :] = nt_dot(cot2, wp[...])
    agrad[main : main + 16, :] = nt_dot(cot_edge[...], wp[...])

    def gelu(at, l):
        z = preact[l, at, :]
        z2 = z * z
        th = jnp.tanh(GELU_C * (z + GELU_A * (z2 * z)))
        cdf = 0.5 * (1.0 + th)
        slope = cdf + (0.5 * z) * (1.0 - th * th) * (GELU_C * (1.0 + 3.0 * GELU_A * z2))
        return z * cdf, (agrad[at, l * 128 : (l + 1) * 128] * slope).astype(BF16)

    tiles = out_cols // 16

    def activate(r, carry):
        for t in range(tiles):
            at = pl.ds(pl.multiple_of(r * out_cols + t * 16, 16), 16)
            for l in range(4):
                lanes = slice(l * 128, (l + 1) * 128)
                a, p = gelu(at, l)
                act[at, lanes] = a.astype(BF16)
                pre[at, lanes] = p
                pre32[l, pl.ds(pl.multiple_of(r * pspan + 8 + t * 16, 8), 16), :] = p.astype(F32)
        return carry

    lax.fori_loop(0, lat, activate, 0)
    for l in range(4):
        edge_pre = gelu(slice(main, main + 16), l)[1].astype(F32)
        pre32[l, pl.ds(7, lat, stride=pspan), :] = edge_pre[0:8]
        pre32[l, pl.ds(8 + out_cols, lat, stride=pspan), :] = edge_pre[8:16]

    def pair(which, p):
        return remote(
            sums.at[which, p, :, 1 - core], crecv.at[which, p], partner, c_sem_s.at[which, p], c_sem_r.at[which, p]
        )

    def send_all(which):
        for p in range(4):
            pair(which, p).wait()

        def one(i, carry):
            at = pl.ds(pl.multiple_of(lax.rem(i, 16) * 8, 8), 8)
            x_hi = i // 16
            even, odd = messages([sums[which, l, x_hi, core, at, :] + crecv[which, l, x_hi, at, :] for l in range(4)])
            msend[which, 2 * i] = even.astype(BF16)
            msend[which, 2 * i + 1] = odd.astype(BF16)
            return carry

        lax.fori_loop(0, 32, one, 0, unroll=4)

        def push(i, carry):
            chip = lax.rem(my_chip + i, chips)
            remote(
                msend.at[which, chip], mrecv.at[which, i - 1], peer(i), m_sem_s.at[which], m_sem_r.at[which]
            ).start()
            return carry

        lax.fori_loop(1, chips, push, 0, unroll=9)

    def collect(which, out_ref):
        everything = pltpu.make_async_copy(
            msend.at[which, 0 : chips - 1], mrecv.at[which], m_sem_r.at[which]
        )
        everything.wait()
        pltpu.make_async_copy(
            msend.at[which, 0 : chips - 1], mrecv.at[which], m_sem_s.at[which]
        ).wait()

        def one(i, carry):
            return carry + mrecv[which, i].astype(F32)

        total = lax.fori_loop(0, chips - 1, one, msend[which, my_chip].astype(F32), unroll=7)
        out_ref[...] = total * scale

    for x_hi in range(2):
        y = dot(cot_t[x_hi * HALF : (x_hi + 1) * HALF, :], act[...])
        for l in range(4):
            for q in range(2):
                sums[0, l, x_hi, q] = y[q * 128 : (q + 1) * 128, l * 128 : (l + 1) * 128]
    pre_t[...] = pre[...].T
    pl.semaphore_wait(barrier, chips)
    for p in range(4):
        pair(0, p).start()

    low_lanes = lax.broadcasted_iota(jnp.int32, (64, 128), 1) < 64

    def conv_grad(p, carry):
        for h in range(2):
            lanes = pl.ds(pl.multiple_of(p * 2 * HALF, 2 * HALF), 2 * HALF)
            both = dot(pre_t[h * HALF : (h + 1) * HALF, :], pt[h, 0:main, lanes])
            for g in range(4):
                rows = slice(g * 64, g * 64 + 64)
                tile = (g // 2) * 128
                a = both[rows, tile : tile + 128]
                b = both[rows, HALF + tile : HALF + tile + 128]
                if g % 2 == 0:
                    b = pltpu.roll(b, 64, 1)
                else:
                    a = pltpu.roll(a, 64, 1)
                half = (g % 2) * 64
                sums[1, p, h, g // 2, half : half + 64, :] = jnp.where(low_lanes, a, b)
        pair(1, p).start()
        return carry

    lax.fori_loop(0, KW // 2, conv_grad, 0)
    send_all(0)
    send_all(1)
    enc[...] = dot(act[...], wp[...]).astype(BF16).reshape(lat, out_cols, C)

    for r in range(lat):
        at = slice(r * out_cols, (r + 1) * out_cols)
        for l in range(4):
            lanes = slice(l * 128, (l + 1) * 128)
            pm[at, lanes] = pre32[l, r * pspan + 7 : r * pspan + 7 + out_cols, :].astype(BF16)
            pp[at, lanes] = pre32[l, r * pspan + 9 : r * pspan + 9 + out_cols, :].astype(BF16)

    gblock = 4

    def input_grad(c, carry):
        rows = gblock * out_cols
        at = pl.ds(pl.multiple_of(c * rows, 16), rows)
        for h in range(2):
            lanes = slice(h * HALF, (h + 1) * HALF)
            here = pre[at, lanes]
            for m, (first, second, shifted) in enumerate(((2, 6, pm), (3, 7, pm), (4, 0, pp), (5, 1, pp))):
                y = nt_dot(here, wd[h, first * HALF : (first + 1) * HALF, :]) + nt_dot(
                    shifted[at, lanes], wd[h, second * HALF : (second + 1) * HALF, :]
                )
                for r in range(gblock):
                    for i in range(2):
                        g32[2 * h + i, pl.ds((c * gblock + r) * cols + m, out_cols, stride=4), :] = y[
                            r * out_cols : (r + 1) * out_cols, i * 128 : (i + 1) * 128
                        ]
        for r in range(gblock):
            row = c * gblock + r
            for s in range(0, cols, 16):
                for l in range(4):
                    gout[row, s : s + 16, l * 128 : (l + 1) * 128] = g32[
                        l, pl.ds(pl.multiple_of(row * cols + s, 16), 16), :
                    ].astype(BF16)
        return carry

    lax.fori_loop(0, lat // gblock, input_grad, 0)

    collect(0, gpoint_ref)
    collect(1, gconv_ref)


def drain_body(enc, gout, conv, point, enc_hbm, gin_hbm, conv_hbm, point_hbm, sems):
    moves = [
        pltpu.make_async_copy(src, dst, sems.at[i])
        for i, (src, dst) in enumerate(
            ((gout, gin_hbm), (enc, enc_hbm), (conv, conv_hbm), (point, point_hbm))
        )
    ]
    for m in moves:
        m.start()
    for m in moves:
        m.wait()


def per_device(n_lat, n_lon, inputs, w_conv, w_point, cotangent):
    lat, cols, channels = inputs.shape
    out_cols = cols // 4
    main = lat * out_cols
    chips = (n_lat // 2) * n_lon
    scale = 1.0 / math.sqrt(main * n_lat * n_lon)
    dma = pltpu.SemaphoreType.DMA
    vmem = pltpu.VMEM
    any_spec = pl.BlockSpec(memory_space=pltpu.HBM)
    vmem_spec = pl.BlockSpec(memory_space=pltpu.VMEM)

    inputs, w_conv, w_point, cotangent = (
        pltpu.with_memory_space_constraint(a, pltpu.HBM) for a in (inputs, w_conv, w_point, cotangent)
    )
    handed = pl.pallas_call(
        functools.partial(open_body, n_lon),
        out_shape=(
            vmem((2, main + 16, KW * HALF), BF16),
            vmem((2, KW * HALF, HALF), BF16),
            vmem((16, C), BF16),
        ),
        in_specs=[any_spec] * 3,
        out_specs=(vmem_spec,) * 3,
        scratch_shapes=[
            vmem((lat, cols, C), BF16),
            vmem((4, lat * (cols + 16), 128), F32),
            vmem((C, C), BF16),
            vmem((lat, 8, C), BF16),
            vmem((lat, 8, C), BF16),
            vmem((lat, 8, C), BF16),
            vmem((lat, 8, C), BF16),
            vmem((4, 2 * lat * 8, 128), F32),
            dma((lat,)),
            dma((1,)),
            dma((4,)),
            dma((4,)),
        ],
        compiler_params=pltpu.CompilerParams(
            collective_id=1, has_side_effects=True, vmem_limit_bytes=32 * 1024 * 1024
        ),
        name="halo_step",
    )(inputs, w_conv, cotangent)

    results = pl.pallas_call(
        functools.partial(close_body, n_lat, n_lon, scale, lat, cols),
        out_shape=(
            vmem((lat, out_cols, C), BF16),
            vmem((lat, cols, C), BF16),
            vmem((16, 128), F32),
            vmem((16, 128), F32),
        ),
        in_specs=[any_spec] * 2 + [vmem_spec] * 3,
        out_specs=(vmem_spec,) * 4,
        scratch_shapes=[
            vmem((C, C), BF16),
            vmem((lat, out_cols, C), BF16),
            vmem((4, main + 16, 128), F32),
            vmem((main + 16, C), F32),
            vmem((C, main), BF16),
            vmem((main, C), BF16),
            vmem((main, C), BF16),
            vmem((C, main), BF16),
            vmem((4, lat * (out_cols + 16), 128), F32),
            vmem((main, C), BF16),
            vmem((main, C), BF16),
            vmem((4, lat * cols, 128), F32),
            vmem((2, 4, 2, 2, 128, 128), F32),
            vmem((2, 4, 2, 128, 128), F32),
            vmem((2, chips, 16, 128), BF16),
            vmem((2, chips - 1, 16, 128), BF16),
            dma((2,)),
            dma((2, 4)),
            dma((2, 4)),
            dma((2,)),
            dma((2,)),
        ],
        compiler_params=pltpu.CompilerParams(
            collective_id=0, has_side_effects=True, vmem_limit_bytes=40 * 1024 * 1024
        ),
        name="layer_step",
    )(w_point, cotangent, *handed)

    encoded, grad_inputs, conv, point = pl.pallas_call(
        drain_body,
        out_shape=(
            jax.ShapeDtypeStruct((lat, out_cols, C), BF16),
            jax.ShapeDtypeStruct((lat, cols, C), BF16),
            jax.ShapeDtypeStruct((16, 128), F32),
            jax.ShapeDtypeStruct((16, 128), F32),
        ),
        in_specs=[vmem_spec] * 4,
        out_specs=(any_spec,) * 4,
        scratch_shapes=[dma((4,))],
        compiler_params=pltpu.CompilerParams(vmem_limit_bytes=8 * 1024 * 1024),
        name="drain",
    )(*results)

    def unfold(block):
        return block.reshape(4, 4, 128).transpose(0, 2, 1).reshape(C, 4)

    return encoded, grad_inputs, unfold(conv), unfold(point)


def solution(mesh):
    placed = (P("lat", "lon", None), P(), P(), P("lat", "lon", None))
    return jax.shard_map(
        functools.partial(per_device, mesh.shape["lat"], mesh.shape["lon"]),
        mesh=mesh,
        in_specs=placed,
        out_specs=(
            P("lat", "lon", None),
            P("lat", "lon", None),
            P(None, ("lat", "lon")),
            P(None, ("lat", "lon")),
        ),
        check_vma=False,
    )
```
